32 devices in a mesh: section: 2 (over x), dp: 4 (over z), mp: 4 (over y, core).
Axes of the slice: x: 2, y: 2, z: 4, core: 2. Of those that a mesh axis runs over, the one named last changes fastest.
Arguments:
- inputs: bfloat16 [3, 576, 4, 1024], P(None, 'mp', 'dp'), may hold values from -6 to 6
- cotangent: bfloat16 [3, 576, 4, 1024], P(None, 'mp', 'dp'), may hold values from -6 to 6
- w_qkv: bfloat16 [2, 1024, 3, 1024], P('section', 'dp', None, 'mp'), may hold values from -0.125 to 0.125
- w_out: bfloat16 [2, 1024, 1024], P('section', 'mp', 'dp'), may hold values from -0.1875 to 0.1875
- w_up: bfloat16 [2, 1024, 4096], P('section', 'dp', 'mp'), may hold values from -0.1875 to 0.1875
- w_down: bfloat16 [2, 4096, 1024], P('section', 'mp', 'dp'), may hold values from -0.09375 to 0.09375
- norm_gains: bfloat16 [2, 2, 1024], P('section', None, 'dp'), may hold values from 0.25 to 1.75
- biases_d: bfloat16 [2, 4, 1024], P('section', None, 'dp'), may hold values from -1.75 to 1.75
- head_bias: bfloat16 [2, 2, 4, 256], P('section', None, 'mp', 'dp'), may hold values from -3 to 3
- hidden_bias: bfloat16 [2, 4, 1024], P('section', 'mp', 'dp'), may hold values from -3 to 3
Outputs:
- acts: bfloat16 [2, 3, 576, 4, 1024], P('section', None, 'mp', 'dp')
- input_grads: float32 [2, 3, 576, 4, 1024], P('section', None, 'mp', 'dp')
- grad_w_qkv: float32 [2, 1024, 3, 1024], P('section', 'dp', None, 'mp')
- grad_w_out: float32 [2, 1024, 1024], P('section', 'mp', 'dp')
- grad_w_up: float32 [2, 1024, 4096], P('section', 'dp', 'mp')
- grad_w_down: float32 [2, 4096, 1024], P('section', 'mp', 'dp')
- grad_norm_gains: float32 [2, 2, 1024], P('section', None, 'dp')
- grad_biases_d: float32 [2, 4, 1024], P('section', None, 'dp')
- grad_head_bias: float32 [2, 2, 4, 256], P('section', None, 'mp', 'dp')
- grad_hidden_bias: float32 [2, 4, 1024], P('section', 'mp', 'dp')
The draws below stay inside these ranges and needn't reach their ends.
All inputs are finite; a program needn't handle non-finite values.
Results may differ from the reference program's by a relative error of at most 0.024.
Values may be sent and summed in bfloat16 or wider, within the bound.
No kernel may reach another device: no remote copies, remote signals or barrier semaphores. Data moves between devices by JAX's collectives and lax.ppermute only.
A program may use at most 192 MiB of HBM per device.

```python
import jax
import jax.numpy as jnp
from jax import lax

D = 1024
HEADS = 16
FF = 4096
HD = 64
SEQ = 576
MICRO = 3
BATCH = 4
N_MP = 4


def draw_inputs(key, part):
    own = jax.random.fold_in(key, 1)
    second_key = jax.random.fold_in(own, 1)
    shape = (MICRO, SEQ, BATCH, D)
    values = jax.random.normal(second_key, shape)
    return jnp.clip(values, -6.0, 6.0).astype(jnp.bfloat16)


def draw_w_qkv(key, part):
    own = jax.random.fold_in(key, 2)
    shape = (2, D, 3, D)
    values = jnp.clip(jax.random.normal(own, shape), -4.0, 4.0) * D ** (-0.5)
    return values.astype(jnp.bfloat16)


def spiked(result, own_key, source, target, parts, factor):
    def block_of(position):
        return (jnp.arange(result.shape[position]) // (result.shape[position] // parts)).reshape((-1,) + (1,) * (result.ndim - 1 - position))

    one_side = jax.random.permutation(own_key, parts)[block_of(target)]
    far = (block_of(target) + parts // 2) % parts
    return jnp.where((block_of(source) == one_side) | (block_of(source) == far), factor * result, result)


def block_levels(stream_key, dims, shards, least, high):
    level, own = 1.0, jax.random.fold_in(stream_key, 6)
    for dim, shards_of in shards:
        heights = jnp.exp(jax.random.uniform(jax.random.fold_in(own, dim), (shards_of,), jnp.float32, least / len(shards), high / len(shards)))
        level = level * jnp.repeat(heights, dims[dim] // shards_of).reshape([-1 if axis == dim else 1 for axis in range(len(dims))])
    return level


def normal_values(stream_key, shape, deviation, most, cuts=(), held_as=jnp.bfloat16):
    values = jax.random.normal(stream_key, shape, jnp.float32) * deviation
    if len(cuts) > 0:
        values = block_levels(stream_key, shape, cuts, -0.22, 0.18) * values
    return jnp.clip(values, min=-most, max=most).astype(held_as)


def gaussian_with(stream_key, extent, spread, most, shards, heavy, held_as=jnp.bfloat16):
    drawn = spread * jax.random.normal(stream_key, extent, jnp.float32)
    if shards:
        drawn = drawn * block_levels(stream_key, extent, shards, -0.22, 0.18)
    return jnp.clip(spiked(drawn, jax.random.fold_in(stream_key, 3), *heavy), -most, most).astype(held_as)


def setup_inputs(seed: int = 0) -> dict:
    streams_of = jax.random.split(jax.random.key(seed), 11)
    return {
        "inputs": draw_inputs(jax.random.fold_in(streams_of[10], 71), 0),
        "cotangent": gaussian_with(streams_of[1], (MICRO, SEQ, BATCH, D), 1.0, 6.0, ((1, 4), (2, 4)), (2, 3, 4, 2.0)),
        "w_qkv": draw_w_qkv(jax.random.fold_in(streams_of[10], 71), 0),
        "w_out": normal_values(streams_of[3], (2, D, D), D ** -0.5, 0.1875, ((0, 2), (1, 4), (2, 4))),
        "w_up": normal_values(streams_of[4], (2, D, FF), D ** -0.5, 0.1875, ((0, 2), (1, 4), (2, 4))),
        "w_down": normal_values(streams_of[5], (2, FF, D), FF ** -0.5, 0.09375, ((0, 2), (1, 4), (2, 4))),
        "norm_gains": jnp.clip(1.0 + 0.15 * jax.random.normal(streams_of[6], (2, 2, D), jnp.float32), 0.25, 1.75).astype(jnp.bfloat16),
        "biases_d": normal_values(streams_of[7], (2, 4, D), 0.3, 1.75, ((0, 2), (2, 4))),
        "head_bias": normal_values(streams_of[8], (2, 2, N_MP, D // N_MP), 0.5, 3.0, ((0, 2), (2, 4), (3, 4))),
        "hidden_bias": normal_values(streams_of[9], (2, N_MP, FF // N_MP), 0.5, 3.0, ((0, 2), (1, 4), (2, 4))),
    }


epsilon = 1e-06
root_half = 0.7071067811865476
inv_root_tau = 0.3989422804014327

def gelu_slope(pre):
    return 0.5 * (1.0 + lax.erf(pre * root_half)) + pre * jnp.exp(-0.5 * pre * pre) * inv_root_tau

def norm_forward(rows, gain, shift):
    average = lax.optimization_barrier(jnp.mean(rows, -1, keepdims=True))
    centred = rows - average
    inverse_std = lax.rsqrt(lax.optimization_barrier(jnp.mean(centred * centred, -1, keepdims=True)) + epsilon)
    unit = centred * inverse_std
    return (unit * gain + shift, unit, inverse_std)

def norm_backward(grad_norm, unit, inverse_std, gain):
    scaled = grad_norm * gain
    return inverse_std * (scaled - lax.optimization_barrier(jnp.mean(scaled, -1, keepdims=True)) - unit * lax.optimization_barrier(jnp.mean(scaled * unit, -1, keepdims=True)))

def split_heads(qkv):
    queries = qkv[:, 0].reshape(SEQ, HEADS, HD).astype(jnp.float32)
    keys_all = qkv[:, 1].reshape(SEQ, HEADS, HD).astype(jnp.float32)
    values = qkv[:, 2].reshape(SEQ, HEADS, HD).astype(jnp.float32)
    return (queries, keys_all, values)

def layer_forward(layer_in, params):
    qkv_w, out_w, up_w, down_w, gains, shifts, head_b, hidden_b = params
    normed1, unit1, inverse1 = norm_forward(layer_in, gains[0], shifts[0])
    normed1 = normed1.astype(jnp.bfloat16)
    bias_rows = jnp.stack([head_b[0], jnp.zeros_like(head_b[0]), head_b[1]])
    qkv = (jnp.einsum('sd,dte->ste', normed1.astype(jnp.float32), qkv_w.astype(jnp.float32)) + bias_rows).astype(jnp.bfloat16)
    queries, keys_all, values = split_heads(qkv)
    scores = jnp.einsum('qhd,khd->hqk', queries, keys_all) * HD ** (-0.5)
    top = lax.optimization_barrier(jnp.max(scores, -1, keepdims=True))
    log_total = top + jnp.log(lax.optimization_barrier(jnp.sum(jnp.exp(scores - top), -1, keepdims=True)))
    probs = jnp.exp(scores - log_total).astype(jnp.bfloat16)
    attended = jnp.einsum('hqk,khd->qhd', probs.astype(jnp.float32), values).astype(jnp.bfloat16).reshape(SEQ, D)
    middle = layer_in + jnp.dot(attended, out_w, preferred_element_type=jnp.float32) + shifts[1]
    normed2, unit2, inverse2 = norm_forward(middle, gains[1], shifts[2])
    normed2 = normed2.astype(jnp.bfloat16)
    pre = jnp.dot(normed2, up_w, preferred_element_type=jnp.float32) + hidden_b
    active = jax.nn.gelu(pre, approximate=False).astype(jnp.bfloat16)
    layer_out = middle + jnp.dot(active, down_w, preferred_element_type=jnp.float32) + shifts[3]
    kept = (unit1, inverse1, normed1, qkv, log_total, attended, unit2, inverse2, normed2, pre, active)
    return (layer_out, kept)

def layer_backward(grad_out, kept, params):
    qkv_w, out_w, up_w, down_w, gains, shifts, head_b, hidden_b = params
    unit1, inverse1, normed1, qkv, log_total, attended, unit2, inverse2, normed2, pre, active = kept
    grad_out_b = grad_out.astype(jnp.bfloat16)
    grad_down = jnp.dot(active.T, grad_out_b, preferred_element_type=jnp.float32)
    grad_pre = (jnp.dot(grad_out_b, down_w.T, preferred_element_type=jnp.float32) * gelu_slope(pre)).astype(jnp.bfloat16)
    grad_up = jnp.dot(normed2.T, grad_pre, preferred_element_type=jnp.float32)
    grad_hidden = lax.optimization_barrier(jnp.sum(grad_pre.astype(jnp.float32), 0))
    grad_norm2 = jnp.dot(grad_pre, up_w.T, preferred_element_type=jnp.float32)
    grad_middle = grad_out + norm_backward(grad_norm2, unit2, inverse2, gains[1])
    grad_middle_b = grad_middle.astype(jnp.bfloat16)
    grad_outw = jnp.dot(attended.T, grad_middle_b, preferred_element_type=jnp.float32)
    grad_att = jnp.dot(grad_middle_b, out_w.T, preferred_element_type=jnp.float32).astype(jnp.bfloat16)
    queries, keys_all, values = split_heads(qkv)
    grad_heads = grad_att.reshape(SEQ, HEADS, HD).astype(jnp.float32)
    scores = jnp.einsum('qhd,khd->hqk', queries, keys_all) * HD ** (-0.5)
    probs_f = jnp.exp(scores - log_total)
    probs_b = probs_f.astype(jnp.bfloat16).astype(jnp.float32)
    grad_values = jnp.einsum('hqk,qhd->khd', probs_b, grad_heads)
    grad_probs = jnp.einsum('qhd,khd->hqk', grad_heads, values)
    inner = lax.optimization_barrier(jnp.sum(probs_f * grad_probs, -1, keepdims=True))
    grad_scores = (probs_f * (grad_probs - inner)).astype(jnp.bfloat16).astype(jnp.float32)
    grad_queries = jnp.einsum('hqk,khd->qhd', grad_scores, keys_all) * HD ** (-0.5)
    grad_keys = jnp.einsum('hqk,qhd->khd', grad_scores, queries) * HD ** (-0.5)
    grad_qkv = jnp.stack([grad_queries, grad_keys, grad_values], 1).reshape(SEQ, 3, D).astype(jnp.bfloat16)
    grad_qkv_f = grad_qkv.astype(jnp.float32)
    grad_qkvw = jnp.einsum('sd,ste->dte', normed1.astype(jnp.float32), grad_qkv_f)
    summed = lax.optimization_barrier(jnp.sum(grad_qkv_f, 0))
    grad_head = jnp.stack([summed[0], summed[2]])
    grad_norm1 = jnp.einsum('ste,dte->sd', grad_qkv_f, qkv_w.astype(jnp.float32))
    grad_in = grad_middle + norm_backward(grad_norm1, unit1, inverse1, gains[0])
    grad_gains = jnp.stack([lax.optimization_barrier(jnp.sum(grad_norm1 * unit1, 0)), lax.optimization_barrier(jnp.sum(grad_norm2 * unit2, 0))])
    grad_shifts = jnp.stack([lax.optimization_barrier(jnp.sum(grad_norm1, 0)), lax.optimization_barrier(jnp.sum(grad_middle, 0)), lax.optimization_barrier(jnp.sum(grad_norm2, 0)), lax.optimization_barrier(jnp.sum(grad_out, 0))])
    return (grad_in, (grad_qkvw, grad_outw, grad_up, grad_down, grad_gains, grad_shifts, grad_head, grad_hidden))

def reference(inputs, cotangent, w_qkv, w_out, w_up, w_down, norm_gains, biases_d, head_bias, hidden_bias):

    def section_params(index):
        return (w_qkv[index], w_out[index], w_up[index], w_down[index], norm_gains[index].astype(jnp.float32), biases_d[index].astype(jnp.float32), head_bias[index].reshape(2, D).astype(jnp.float32), hidden_bias[index].reshape(FF).astype(jnp.float32))
    first_params = section_params(0)
    second_params = section_params(1)
    images = inputs.transpose(0, 2, 1, 3).reshape(MICRO * BATCH, SEQ, D)
    targets = cotangent.transpose(0, 2, 1, 3).reshape(MICRO * BATCH, SEQ, D)
    zero_grads = (jnp.zeros((D, 3, D), jnp.float32), jnp.zeros((D, D), jnp.float32), jnp.zeros((D, FF), jnp.float32), jnp.zeros((FF, D), jnp.float32), jnp.zeros((2, D), jnp.float32), jnp.zeros((4, D), jnp.float32), jnp.zeros((2, D), jnp.float32), jnp.zeros((FF,), jnp.float32))

    def one_image(carry, item):
        image, target = item
        out_first, kept_first = layer_forward(image.astype(jnp.float32), first_params)
        handed = out_first.astype(jnp.bfloat16)
        out_second, kept_second = layer_forward(handed.astype(jnp.float32), second_params)
        grad_second, grads_second = layer_backward(target.astype(jnp.float32), kept_second, second_params)
        grad_first, grads_first = layer_backward(grad_second, kept_first, first_params)
        total_first = jax.tree.map(lambda left, right: left + right, carry[0], grads_first)
        total_second = jax.tree.map(lambda left, right: left + right, carry[1], grads_second)
        return ((total_first, total_second), (handed, out_second.astype(jnp.bfloat16), grad_first, grad_second))
    totals, results = lax.scan(one_image, (zero_grads, zero_grads), (images, targets))

    def restore(stacked):
        return stacked.reshape(MICRO, BATCH, SEQ, D).transpose(0, 2, 1, 3)
    acts = jnp.stack([restore(results[0]), restore(results[1])])
    input_grads = jnp.stack([restore(results[2]), restore(results[3])])
    joined = [jnp.stack([left, right]) for left, right in zip(totals[0], totals[1])]
    grad_head = joined[6].reshape(2, 2, N_MP, D // N_MP)
    grad_hidden = joined[7].reshape(2, N_MP, FF // N_MP)
    return (acts, input_grads, joined[0], joined[1], joined[2], joined[3], joined[4], joined[5], grad_head, grad_hidden)
```

```python
import functools

import jax
import jax.numpy as jnp
from jax import lax
from jax.experimental import pallas as pl
from jax.experimental.pallas import tpu as pltpu
from jax.sharding import PartitionSpec as P

HD = 64
epsilon = 1e-06
root_half = 0.7071067811865476
inv_root_tau = 0.3989422804014327
bf = jnp.bfloat16
f32 = jnp.float32


def dot(a, b, ca=1, cb=0):
    return lax.dot_general(a, b, (((ca,), (cb,)), ((), ())), preferred_element_type=f32)


def params_of(limit=48):
    return pltpu.CompilerParams(vmem_limit_bytes=limit << 20)


def shape(dims, dtype):
    return jax.ShapeDtypeStruct(dims, dtype)


def attn_fwd_kernel(n_ref, w_ref, b_ref, own_ref, oth_ref, qkv_ref, lse_ref, att_ref):
    width = b_ref.shape[1] // 3
    part = own_ref.shape[0]
    qkv = dot(n_ref[...], w_ref[:, : 3 * width]) + b_ref[...]
    qkv_b = qkv.astype(bf)
    qkv_ref[...] = qkv_b
    q = qkv_b[:, :width] * jnp.asarray(HD**-0.5, bf)
    k = qkv_b[:, width : 2 * width]
    v = qkv_b[:, 2 * width :]
    lane = lax.broadcasted_iota(jnp.int32, (1, width), 1) // HD
    row = lax.broadcasted_iota(jnp.int32, (width, 1), 0) // HD
    out = None
    for head in range(width // HD):
        keys = jnp.where(lane == head, k, jnp.zeros_like(k))
        scores = dot(keys, q, 1, 1)
        top = jnp.max(scores, 0, keepdims=True)
        raised = jnp.exp(scores - top)
        total = jnp.sum(raised, 0, keepdims=True)
        lse_ref[head : head + 1, :] = top + jnp.log(total)
        mixed = dot(v, raised.astype(bf), 0, 0) / total
        out = mixed if out is None else jnp.where(row == head, mixed, out)
    att = out.T.astype(bf)
    att_ref[...] = att
    term = dot(att, w_ref[:, 3 * width :], 1, 1)
    own_ref[...] = term[:part]
    oth_ref[...] = term[part:].astype(bf)


def attn_fwd(full, weights, bias):
    rows, model = full.shape
    width = bias.shape[1] // 3
    return pl.pallas_call(
        attn_fwd_kernel,
        name="attn_fwd",
        out_shape=(
            shape((rows // 2, model), f32),
            shape((rows // 2, model), bf),
            shape((rows, 3 * width), bf),
            shape((width // HD, rows), f32),
            shape((rows, width), bf),
        ),
        compiler_params=params_of(),
        cost_estimate=pl.CostEstimate(flops=1_500_000_000, bytes_accessed=5_000_000, transcendentals=700_000),
    )(full, weights, bias)


def attn_bwd_kernel(g_ref, w_ref, qkv_ref, lse_ref, own_ref, oth_ref, gqkv_ref, sum_ref):
    width = qkv_ref.shape[1] // 3
    part = own_ref.shape[0]
    ga = dot(g_ref[...], w_ref[:, 3 * width :]).astype(bf)
    qkv_b = qkv_ref[...]
    scale = HD**-0.5
    q = qkv_b[:, :width] * jnp.asarray(scale, bf)
    k = qkv_b[:, width : 2 * width]
    v = qkv_b[:, 2 * width :]
    lane = lax.broadcasted_iota(jnp.int32, (1, width), 1) // HD
    row = lax.broadcasted_iota(jnp.int32, (width, 1), 0) // HD
    gq = gk = gv = None
    for head in range(width // HD):
        mine = lane == head
        keys = jnp.where(mine, k, jnp.zeros_like(k))
        gah = jnp.where(mine, ga, jnp.zeros_like(ga))
        probs = jnp.exp(dot(keys, q, 1, 1) - lse_ref[head : head + 1, :])
        gv_h = dot(probs.astype(bf), ga)
        gprobs = dot(v, gah, 1, 1)
        inner = jnp.sum(probs * gprobs, 0, keepdims=True)
        gs = (probs * (gprobs - inner)).astype(bf)
        gk_h = dot(gs, q)
        gq_h = dot(k, gs, 0, 0)
        if gq is None:
            gq, gk, gv = gq_h, gk_h, gv_h
        else:
            gq = jnp.where(row == head, gq_h, gq)
            gk = jnp.where(mine, gk_h, gk)
            gv = jnp.where(mine, gv_h, gv)
    gqkv = jnp.concatenate([(gq.T * scale).astype(bf), gk.astype(bf), gv.astype(bf)], 1)
    gqkv_ref[...] = gqkv
    sum_ref[...] = jnp.sum(gqkv.astype(f32), 0, keepdims=True)
    term = dot(gqkv, w_ref[:, : 3 * width], 1, 1)
    own_ref[...] = term[:part]
    oth_ref[...] = term[part:].astype(bf)


def attn_bwd(full, weights, qkv, lse):
    rows, model = full.shape
    return pl.pallas_call(
        attn_bwd_kernel,
        name="attn_bwd",
        out_shape=(
            shape((rows // 2, model), f32),
            shape((rows // 2, model), bf),
            shape(qkv.shape, bf),
            shape((1, qkv.shape[1]), f32),
        ),
        compiler_params=params_of(),
        cost_estimate=pl.CostEstimate(flops=2_500_000_000, bytes_accessed=5_000_000, transcendentals=700_000),
    )(full, weights, qkv, lse)


def mlp_fwd_kernel(n_ref, w_ref, b_ref, own_ref, oth_ref, act_ref, slope_ref):
    hidden = b_ref.shape[1]
    part = own_ref.shape[0]
    pre = dot(n_ref[...], w_ref[:, :hidden]) + b_ref[...]
    phi = 0.5 * (1.0 + lax.erf(pre * root_half))
    act = (pre * phi).astype(bf)
    act_ref[...] = act
    slope_ref[...] = phi + pre * jnp.exp(-0.5 * pre * pre) * inv_root_tau
    term = dot(act, w_ref[:, hidden:], 1, 1)
    own_ref[...] = term[:part]
    oth_ref[...] = term[part:].astype(bf)


def mlp_fwd(full, weights, bias):
    rows, model = full.shape
    hidden = bias.shape[1]
    return pl.pallas_call(
        mlp_fwd_kernel,
        name="mlp_fwd",
        out_shape=(
            shape((rows // 2, model), f32),
            shape((rows // 2, model), bf),
            shape((rows, hidden), bf),
            shape((rows, hidden), f32),
        ),
        compiler_params=params_of(),
        cost_estimate=pl.CostEstimate(flops=1_300_000_000, bytes_accessed=7_000_000, transcendentals=700_000),
    )(full, weights, bias)


def mlp_bwd_kernel(g_ref, w_ref, slope_ref, own_ref, oth_ref, gp_ref, sum_ref):
    hidden = slope_ref.shape[1]
    part = own_ref.shape[0]
    gp = (dot(g_ref[...], w_ref[:, hidden:]) * slope_ref[...]).astype(bf)
    gp_ref[...] = gp
    sum_ref[...] = jnp.sum(gp.astype(f32), 0, keepdims=True)
    term = dot(gp, w_ref[:, :hidden], 1, 1)
    own_ref[...] = term[:part]
    oth_ref[...] = term[part:].astype(bf)


def mlp_bwd(full, weights, slope):
    rows, model = full.shape
    hidden = slope.shape[1]
    return pl.pallas_call(
        mlp_bwd_kernel,
        name="mlp_bwd",
        out_shape=(
            shape((rows // 2, model), f32),
            shape((rows // 2, model), bf),
            shape((rows, hidden), bf),
            shape((1, hidden), f32),
        ),
        compiler_params=params_of(),
        cost_estimate=pl.CostEstimate(flops=1_300_000_000, bytes_accessed=7_000_000, transcendentals=0),
    )(full, weights, slope)


def grads_kernel(count, *refs):
    out_ref = refs[-1]
    for side in range(2):
        total = None
        for index in range(count):
            left, right = refs[(side * count + index) * 2 : (side * count + index) * 2 + 2]
            term = dot(left[...], right[...], 0, 0)
            total = term if total is None else total + term
        width = total.shape[1]
        if side == 0:
            out_ref[:, :width] = total.astype(bf)
        else:
            out_ref[:, out_ref.shape[1] - width :] = total.astype(bf)


def weight_grads(first, second):
    count = len(first)
    rows, model = first[0][0].shape
    columns = first[0][1].shape[1] + second[0][1].shape[1]
    block = 256
    operands, specs = [], []
    for left, right in list(first) + list(second):
        operands += [left, right]
        specs += [
            pl.BlockSpec((rows, block), lambda i: (0, i)),
            pl.BlockSpec(right.shape, lambda i: (0, 0)),
        ]
    return pl.pallas_call(
        functools.partial(grads_kernel, count),
        name="weight_grads",
        grid=(model // block,),
        in_specs=specs,
        out_specs=pl.BlockSpec((block, columns), lambda i: (i, 0)),
        out_shape=shape((model, columns), bf),
        compiler_params=params_of(),
        cost_estimate=pl.CostEstimate(
            flops=2 * count * rows * model * columns,
            bytes_accessed=2 * count * rows * (2 * model + columns),
            transcendentals=0,
        ),
    )(*operands)


def swap(value, axis, bit):
    return lax.ppermute(value, axis, [(i, i ^ bit) for i in range(lax.axis_size(axis))])


def gather_rows(local):
    pair = jnp.concatenate([local, swap(local, "mp", 2)], 0)
    return jnp.concatenate([pair, swap(pair, "mp", 1)], 0)


def sum_rows(own, other, one_way=None):
    chip = own + swap(other, "mp", 1).astype(f32)
    part = chip.shape[0] // 2
    plane = chip[:part] + swap(chip[part:].astype(bf), "mp", 2).astype(f32)
    if one_way is None:
        return plane + swap(plane.astype(bf), "section", 1).astype(f32)
    return plane + lax.ppermute(plane.astype(bf), "section", [one_way]).astype(f32)


def norm_unit(rows):
    average = jnp.mean(rows, -1, keepdims=True)
    centred = rows - average
    inverse_std = lax.rsqrt(jnp.mean(centred * centred, -1, keepdims=True) + epsilon)
    return (centred * inverse_std, inverse_std)


def norm_backward(grad_norm, unit, inverse_std, gain):
    scaled = grad_norm * gain
    return inverse_std * (
        scaled
        - jnp.mean(scaled, -1, keepdims=True)
        - unit * jnp.mean(scaled * unit, -1, keepdims=True)
    )


def body(
    inputs, cotangent, w_qkv, w_out, w_up, w_down, norm_gains, biases_d, head_bias, hidden_bias
):
    section = lax.axis_index("section")
    low = section == 0
    shards = lax.axis_size("dp")
    micro, rows, _, model = inputs.shape
    deep = w_qkv.shape[1]
    width = w_qkv.shape[3] // 2
    hidden = w_up.shape[2] // 2

    qkv_own = w_qkv[0].reshape(deep, 3, 2, width)
    out_own = w_out[0].T
    up_own = w_up[0]
    down_own = w_down[0].T

    def attn_half(half):
        return jnp.concatenate(
            [
                qkv_own[:, 0, half],
                qkv_own[:, 1, half],
                qkv_own[:, 2, half],
                out_own[:, half * width : (half + 1) * width],
            ],
            1,
        )

    def mlp_half(half):
        return jnp.concatenate(
            [
                up_own[:, half * hidden : (half + 1) * hidden],
                down_own[:, half * hidden : (half + 1) * hidden],
            ],
            1,
        )

    def spread(halves):
        to_high = lax.ppermute(halves[1], "section", [(0, 1)])
        to_low = lax.ppermute(halves[0], "section", [(1, 0)])
        return (jnp.where(low, halves[0], to_high), jnp.where(low, to_low, halves[1]))

    attn_parts = spread((attn_half(0), attn_half(1)))
    mlp_parts = spread((mlp_half(0), mlp_half(1)))

    head_row = head_bias[0, :, 0, :].reshape(1, -1)
    head_row = jnp.pad(head_row, ((0, 0), (0, deep - head_row.shape[1])))
    small = jnp.concatenate([norm_gains[0], biases_d[0], hidden_bias[0], head_row], 0)
    small = lax.all_gather(small, ("section", "dp"), axis=0, tiled=False)
    small = small.reshape(2, shards, 8, deep)

    layers = []
    for layer in range(2):
        lines = small[layer].transpose(1, 0, 2).reshape(8, shards * deep).astype(f32)
        heads = small[layer][:, 7, : 4 * width // shards].reshape(shards, 2, -1)
        heads = heads.transpose(1, 0, 2).reshape(2, 2, width).astype(f32)
        heads = jnp.where(low, heads[:, 0], heads[:, 1])
        bias_qkv = jnp.concatenate([heads[0], jnp.zeros_like(heads[0]), heads[1]])[None]
        hid = lines[6].reshape(2, hidden)
        layers.append(
            dict(
                gains=lines[0:2],
                shifts=lines[2:6],
                qkv_bias=bias_qkv,
                hidden_bias=jnp.where(low, hid[0:1], hid[1:2]),
                attn=lax.all_gather(attn_parts[layer], "dp", axis=0, tiled=True),
                mlp=lax.all_gather(mlp_parts[layer], "dp", axis=0, tiled=True),
            )
        )

    acts = [[None] * micro for _ in range(2)]
    kept = [[None] * micro for _ in range(2)]
    stream = [inputs[index, :, 0, :] for index in range(micro)]
    for layer in range(2):
        p = layers[layer]
        gains, shifts = p["gains"], p["shifts"]
        for index in range(micro):
            source = stream[index]
            layer_in = source.astype(f32)
            unit1, inverse1 = norm_unit(layer_in)
            if layer == 0:
                whole = gather_rows(source).astype(f32)
                full1 = (norm_unit(whole)[0] * gains[0] + shifts[0]).astype(bf)
            else:
                full1 = gather_rows((unit1 * gains[0] + shifts[0]).astype(bf))
            own, other, qkv, lse, att = attn_fwd(full1, p["attn"], p["qkv_bias"])
            middle = layer_in + sum_rows(own, other) + shifts[1]
            unit2, inverse2 = norm_unit(middle)
            full2 = gather_rows((unit2 * gains[1] + shifts[2]).astype(bf))
            own, other, act, slope = mlp_fwd(full2, p["mlp"], p["hidden_bias"])
            total = sum_rows(own, other, None if layer == 0 else (0, 1))
            layer_out = (middle + total + shifts[3]).astype(bf)
            acts[layer][index] = layer_out
            stream[index] = layer_out
            kept[layer][index] = (
                unit1, inverse1, full1, qkv, lse, att, unit2, inverse2, full2, act, slope,
            )

    grads_in = [[None] * micro for _ in range(2)]
    packs = [None, None]
    vectors = [None, None]
    heads_sums = [None, None]
    for layer in (1, 0):
        p = layers[layer]
        gains = p["gains"]
        lists = [[], [], [], []]
        vector_total = None
        hidden_total = None
        head_total = None
        for index in range(micro):
            unit1, inverse1, full1, qkv, lse, att, unit2, inverse2, full2, act, slope = kept[layer][
                index
            ]
            if layer == 1:
                grad_b = cotangent[index, :, 0, :]
                grad_out = grad_b.astype(f32)
            else:
                grad_out = grads_in[1][index]
                grad_b = grad_out.astype(bf)
            full_grad = gather_rows(grad_b)
            own, other, gp, gp_sum = mlp_bwd(full_grad, p["mlp"], slope)
            grad_norm2 = sum_rows(own, other)
            grad_middle = grad_out + norm_backward(grad_norm2, unit2, inverse2, gains[1])
            full_middle = gather_rows(grad_middle.astype(bf))
            own, other, gqkv, gqkv_sum = attn_bwd(full_middle, p["attn"], qkv, lse)
            grad_norm1 = sum_rows(own, other, None if layer == 1 else (1, 0))
            grads_in[layer][index] = grad_middle + norm_backward(
                grad_norm1, unit1, inverse1, gains[0]
            )
            lists[0].append((full2, gp))
            lists[1].append((full_grad, act))
            lists[2].append((full1, gqkv))
            lists[3].append((full_middle, att))
            vector = jnp.stack(
                [
                    jnp.sum(grad_norm1 * unit1, 0),
                    jnp.sum(grad_norm2 * unit2, 0),
                    jnp.sum(grad_norm1, 0),
                    jnp.sum(grad_middle, 0),
                    jnp.sum(grad_norm2, 0),
                    jnp.sum(grad_out, 0),
                ]
            )
            vector_total = vector if vector_total is None else vector_total + vector
            hidden_total = gp_sum if hidden_total is None else hidden_total + gp_sum
            head_total = gqkv_sum if head_total is None else head_total + gqkv_sum
        mlp_grads = lax.psum_scatter(
            weight_grads(lists[0], lists[1]), "dp", scatter_dimension=0, tiled=True
        )
        attn_grads = lax.psum_scatter(
            weight_grads(lists[2], lists[3]), "dp", scatter_dimension=0, tiled=True
        )
        packs[layer] = (attn_grads, mlp_grads)
        vectors[layer] = vector_total
        heads_sums[layer] = jnp.concatenate([hidden_total, head_total], 1)

    def collect(first, second):
        to_low = lax.ppermute(first, "section", [(1, 0)])
        to_high = lax.ppermute(second, "section", [(0, 1)])
        return (jnp.where(low, first, to_high), jnp.where(low, to_low, second))

    attn_low, attn_high = collect(packs[0][0], packs[1][0])
    mlp_low, mlp_high = collect(packs[0][1], packs[1][1])
    grad_qkv = jnp.concatenate(
        [
            attn_low[:, : 3 * width].reshape(deep, 3, width),
            attn_high[:, : 3 * width].reshape(deep, 3, width),
        ],
        2,
    ).astype(f32)
    grad_outw = jnp.concatenate([attn_low[:, 3 * width :], attn_high[:, 3 * width :]], 1).T.astype(f32)
    grad_up = jnp.concatenate([mlp_low[:, :hidden], mlp_high[:, :hidden]], 1).astype(f32)
    grad_down = jnp.concatenate([mlp_low[:, hidden:], mlp_high[:, hidden:]], 1).T.astype(f32)

    sums_low, sums_high = collect(heads_sums[0], heads_sums[1])
    vector = jnp.where(low, vectors[0], vectors[1])
    vector = vector + swap(vector, "mp", 1)
    vector = vector + swap(vector, "mp", 2)
    hidden_line = jnp.concatenate([sums_low[:, :hidden], sums_high[:, :hidden]], 1)
    head_lines = []
    for offset in (hidden, hidden + 2 * width):
        head_lines.append(
            jnp.concatenate(
                [sums_low[0, offset : offset + width], sums_high[0, offset : offset + width]]
            ).reshape(shards, -1)
        )
    head_line = jnp.concatenate(head_lines, 1)
    head_line = jnp.pad(head_line, ((0, 0), (0, deep - head_line.shape[1]))).reshape(1, -1)
    lines = jnp.concatenate([vector, hidden_line, head_line], 0)
    place = lax.axis_index("dp")

    def piece(owner):
        return lax.dynamic_slice(lines, (0, owner * deep), (8, deep))

    mine = piece(place)
    for step in range(1, shards):
        moved = piece(lax.rem(place + step, shards))
        mine = mine + lax.ppermute(
            moved, "dp", [(i, (i + step) % shards) for i in range(shards)]
        )
    per_head = 2 * width // shards
    grad_head = mine[7, : 2 * per_head].reshape(1, 2, 1, per_head)

    acts_out = jnp.stack([jnp.where(low, acts[0][i], acts[1][i]) for i in range(micro)])
    grads_out = jnp.stack([jnp.where(low, grads_in[0][i], grads_in[1][i]) for i in range(micro)])
    return (
        acts_out[None, :, :, None, :],
        grads_out[None, :, :, None, :],
        grad_qkv[None],
        grad_outw[None],
        grad_up[None],
        grad_down[None],
        mine[None, 0:2],
        mine[None, 2:6],
        grad_head,
        mine[None, 6:7],
    )


def solution(mesh):
    return jax.shard_map(
        body,
        mesh=mesh,
        in_specs=(
            P(None, "mp", "dp", None),
            P(None, "mp", "dp", None),
            P("section", "dp", None, "mp"),
            P("section", "mp", "dp"),
            P("section", "dp", "mp"),
            P("section", "mp", "dp"),
            P("section", None, "dp"),
            P("section", None, "dp"),
            P("section", None, "mp", "dp"),
            P("section", "mp", "dp"),
        ),
        out_specs=(
            P("section", None, "mp", "dp", None),
            P("section", None, "mp", "dp", None),
            P("section", "dp", None, "mp"),
            P("section", "mp", "dp"),
            P("section", "dp", "mp"),
            P("section", "mp", "dp"),
            P("section", None, "dp"),
            P("section", None, "dp"),
            P("section", None, "mp", "dp"),
            P("section", "mp", "dp"),
        ),
        check_vma=False,
    )
```
